128 devices in a mesh: rows: 32 (over y_hi, z, x), batch: 4 (over y_lo, core).
Axes of the slice: x: 4, y: 4 (y_hi: 2, y_lo: 2; y = y_hi * 2 + y_lo), z: 4, core: 2. Of those that a mesh axis runs over, the one named last changes fastest.
Arguments:
- features: bfloat16 [4, 256, 128, 256], P('batch', 'rows'), may hold values from -6 to 6
- kernels: bfloat16 [3, 3, 3, 256, 256], replicated, may hold values from -0.125 to 0.125
- cotangent: bfloat16 [4, 256, 128, 256], P('batch', 'rows'), may hold values from -6 to 6
Outputs:
- result: bfloat16 [4, 256, 128, 256], P('batch', 'rows')
- grad_features: bfloat16 [4, 256, 128, 256], P('batch', 'rows')
- grad_kernels: float32 [3, 3, 3, 256, 256], replicated
The draws below stay inside these ranges and needn't reach their ends.
All inputs are finite; a program needn't handle non-finite values.
Results may differ from the reference program's by a relative error of at most 0.0065.
Values may be sent and summed in bfloat16 or wider, within the bound.
No kernel may reach another device: no remote copies, remote signals or barrier semaphores. Data moves between devices by JAX's collectives and lax.ppermute only.
A program may use at most 128 MiB of HBM per device.

```python
import math
import jax
import jax.numpy as jnp
from jax import lax

C = 256
BAND = 8
W = 128
H = 256
B = 4


def level_of(rng, extent, cuts, smallest, top_value):
    level, own = 1.0, jax.random.fold_in(rng, 6)
    for position, parts in cuts:
        heights = jnp.exp(jax.random.uniform(jax.random.fold_in(own, position), (parts,), jnp.float32, smallest / len(cuts), top_value / len(cuts)))
        level = level * jnp.repeat(heights, extent[position] // parts).reshape([-1 if axis == position else 1 for axis in range(len(extent))])
    return level


def gaussian(stream_key, dims, spread, reach, shards=(), held_as=jnp.bfloat16):
    entries = jax.random.normal(stream_key, dims, jnp.float32) * spread
    if len(shards) > 0:
        entries = level_of(stream_key, dims, shards, -0.22, 0.18) * entries
    return jnp.clip(entries, min=-reach, max=reach).astype(held_as)


def setup_inputs(seed: int = 0) -> dict:
    seeds = jax.random.split(jax.random.key(seed), 4)
    features = gaussian(seeds[0], (B, H, W, C), 1.0, 6.0, ((0, 4), (1, 32)))
    kernels = gaussian(seeds[1], (3, 3, 3, C, C), (9 * C) ** -0.5, 0.125)
    cotangent = gaussian(seeds[2], (B, H, W, C), 1.0, 6.0, ((0, 4), (1, 32)))
    return dict(features=features, kernels=kernels, cotangent=cotangent)


def convolve(signal, kernel, dilation):
    return lax.conv_general_dilated(signal, kernel, (1, 1), ((dilation, dilation), (dilation, dilation)), rhs_dilation=(dilation, dilation), dimension_numbers=('NHWC', 'HWIO', 'NHWC'), precision=lax.Precision.HIGHEST)

def activate(values):
    values = values.astype(jnp.float32)
    normed = values * lax.rsqrt(lax.optimization_barrier(jnp.mean(values * values, axis=-1, keepdims=True)) + 1e-05)
    return normed * jax.nn.sigmoid(normed)

def reference(features, kernels, cotangent):
    dilations = [4 * BAND, 8 * BAND, 16 * BAND]
    inputs = []
    current = features
    for layer in range(3):
        inputs.append(current)
        signal = activate(current).astype(jnp.bfloat16)
        conv_out = convolve(signal.astype(jnp.float32), kernels[layer].astype(jnp.float32), dilations[layer])
        current = (current.astype(jnp.float32) + conv_out).astype(jnp.bfloat16)
    result = current
    factor = 1.0 / math.sqrt(features.shape[0] * features.shape[1] * features.shape[2])
    grad_flow = cotangent
    kernel_grads = [None, None, None]
    for layer in [2, 1, 0]:
        signal = lax.optimization_barrier(activate(inputs[layer]).astype(jnp.bfloat16)).astype(jnp.float32)
        dilation = dilations[layer]
        _, pull = jax.vjp(lambda sig, ker: convolve(sig, ker, dilation), signal, kernels[layer].astype(jnp.float32))
        dsignal, dkernel = pull(grad_flow.astype(jnp.float32))
        kernel_grads[layer] = dkernel * factor
        _, back = jax.vjp(activate, inputs[layer].astype(jnp.float32))
        dinput, = back(dsignal)
        grad_flow = (grad_flow.astype(jnp.float32) + dinput).astype(jnp.bfloat16)
    return (result, grad_flow, jnp.stack(kernel_grads))
```

```python
import functools
import math

import jax
import jax.numpy as jnp
from jax import lax
from jax.experimental import pallas as pl
from jax.experimental.pallas import tpu as pltpu
from jax.sharding import Mesh
from jax.sharding import PartitionSpec as P


GROUP = ("yh", "z")
CHIPS = ("yh", "z", "x", "yl")
BF16 = jnp.bfloat16
F32 = jnp.float32
PAD = 64
ROWS = 128
UNROLL = 2
VMEM = pl.BlockSpec(memory_space=pltpu.VMEM)
SMEM = pl.BlockSpec(memory_space=pltpu.SMEM)


def taps_of(layer, width):
    return [c for c in range(3) if abs(c - 1) * (32 << layer) < width]


def slots_of(layers, width):
    order = [(l, a, c) for l in layers for a in range(3) for c in taps_of(l, width)]
    return {tap: place for place, tap in enumerate(order)}


def chunk_rows(layers, width):
    rows = 256 * len(slots_of(layers, width))
    return -(-rows // 512) * 512


def blocks(Q, W, body):
    per_q = W // ROWS

    def step(i, carry):
        body(i // per_q, pl.multiple_of((i % per_q) * ROWS, ROWS))
        return carry

    lax.fori_loop(0, Q * per_q, step, 0, unroll=UNROLL)


def normed(x):
    x = x.astype(F32)
    r = lax.rsqrt(jnp.mean(x * x, axis=-1, keepdims=True) + 1e-05)
    n = x * r
    return r, n, 0.5 + 0.5 * jnp.tanh(0.5 * n)


def signal_of(x):
    _, n, s = normed(x)
    return (n * s).astype(BF16)


def clear_pads(buf, Q, W, C):
    zeros = jnp.zeros((Q, PAD, C), BF16)
    buf[:, 0:PAD, :] = zeros
    buf[:, PAD + W :, :] = zeros


def forward_kernel(x_ref, k_ref, res_ref, x1, x2, st, spad, acc):
    Q, W, C = x_ref.shape
    clear_pads(spad, Q, W, C)
    xs = [x_ref, x1, x2]

    def activate(q, j):
        spad[q, pl.ds(PAD + j, ROWS), :] = signal_of(x_ref[q, pl.ds(j, ROWS), :])

    blocks(Q, W, activate)
    for layer in range(3):
        D = 1 << layer
        for a in (1, 0, 2):
            dq = (a - 1) * D
            q0, nq = max(0, -dq), Q - abs(dq)
            total = None
            for c in taps_of(layer, W):
                j0 = PAD + (c - 1) * 32 * D
                lhs = spad[q0 + dq : q0 + dq + nq, j0 : j0 + W, :].reshape(nq * W, C)
                term = jnp.dot(lhs, k_ref[layer, a, c], preferred_element_type=F32)
                total = term if total is None else total + term
            total = total.reshape(nq, W, C)
            if a == 1:
                acc[...] = total
            else:
                acc[q0 : q0 + nq] += total
        for q in range(Q):
            st[layer, :, q * W : (q + 1) * W] = jnp.transpose(spad[q, PAD : PAD + W, :])

        def update(q, j, layer=layer):
            x = xs[layer][q, pl.ds(j, ROWS), :].astype(F32)
            new = (x + acc[q, pl.ds(j, ROWS), :]).astype(BF16)
            if layer < 2:
                xs[layer + 1][q, pl.ds(j, ROWS), :] = new
                spad[q, pl.ds(PAD + j, ROWS), :] = signal_of(new)
            else:
                res_ref[q, pl.ds(j, ROWS), :] = new

        blocks(Q, W, update)


def shifted_grad(gpad, layer, a, c, W, C):
    Q = gpad.shape[0]
    dq = (a - 1) << layer
    q0, nq = max(0, dq), Q - abs(dq)
    j0 = PAD - (c - 1) * (32 << layer)
    return q0, nq, gpad[q0 - dq : q0 - dq + nq, j0 : j0 + W, :].reshape(nq * W, C)


def weight_grads(factor, layer, slots, first, st, gpad, keep_ref, send_ref, W, C):
    half = C // 2
    for a in range(3):
        for c in taps_of(layer, W):
            q0, nq, shifted = shifted_grad(gpad, layer, a, c, W, C)
            grad = jnp.dot(st[layer, :, q0 * W : (q0 + nq) * W], shifted,
                           preferred_element_type=F32) * factor
            keep = jnp.where(first, grad[:half], grad[half:])
            send = jnp.where(first, grad[half:], grad[:half]).astype(BF16)
            row = slots[layer, a, c] * 256
            keep_ref[row : row + half, :] = keep[:, :128]
            keep_ref[row + half : row + 256, :] = keep[:, 128:]
            send_ref[row : row + half, :] = send[:, :128]
            send_ref[row + half : row + 256, :] = send[:, 128:]


def signal_grads(layer, gpad, k_ref, acc, W, C):
    for a in (1, 0, 2):
        total = None
        for c in taps_of(layer, W):
            q0, nq, shifted = shifted_grad(gpad, layer, a, c, W, C)
            term = lax.dot_general(shifted, k_ref[layer, a, c], (((1,), (1,)), ((), ())),
                                   preferred_element_type=F32)
            total = term if total is None else total + term
        total = total.reshape(nq, W, C)
        if a == 1:
            acc[...] = total
        else:
            acc[q0 : q0 + nq] += total


def pulled(x, acc, g):
    r, n, s = normed(x)
    dn = acc * (s * (1.0 + n * (1.0 - s)))
    dx = r * (dn - n * jnp.mean(n * dn, axis=-1, keepdims=True))
    return (g.astype(F32) + dx).astype(BF16)


def clear_tail(slots, keep_ref, send_ref):
    used = 256 * len(slots)
    rest = keep_ref.shape[0] - used
    if rest:
        keep_ref[used:, :] = jnp.zeros((rest, 128), F32)
        send_ref[used:, :] = jnp.zeros((rest, 128), BF16)


def gather_pieces(place_ref, pieces, dest, W):
    Q = len(pieces)
    for k, piece in enumerate(pieces):
        q = lax.rem(place_ref[0] + (Q - k), Q)
        dest[q, PAD : PAD + W, :] = piece[...]


def backward_kernel(factor, core_ref, place_ref, *refs):
    pieces, (x1, x2, st, k_ref, next_ref, keep_ref, send_ref, gpad, acc) = refs[:8], refs[8:]
    Q, W, C = x1.shape
    clear_pads(gpad, Q, W, C)
    gather_pieces(place_ref, pieces, gpad, W)
    first = core_ref[0] == 0
    slots = slots_of((1, 2), W)
    clear_tail(slots, keep_ref, send_ref)
    for layer in (2, 1):
        signal_grads(layer, gpad, k_ref, acc, W, C)
        weight_grads(factor, layer, slots, first, st, gpad, keep_ref, send_ref, W, C)
        xl = x2 if layer == 2 else x1

        def pull(q, j, layer=layer, xl=xl):
            inner = (q, pl.ds(PAD + j, ROWS), slice(None))
            outer = (q, pl.ds(j, ROWS), slice(None))
            new = pulled(xl[outer], acc[outer], gpad[inner])
            if layer == 2:
                gpad[inner] = new
            else:
                next_ref[outer] = new

        blocks(Q, W, pull)


def weights_kernel(factor, core_ref, g_ref, st, keep_ref, send_ref, gpad):
    Q, W, C = g_ref.shape
    clear_pads(gpad, Q, W, C)
    gpad[:, PAD : PAD + W, :] = g_ref[...]
    slots = slots_of((0,), W)
    clear_tail(slots, keep_ref, send_ref)
    weight_grads(factor, 0, slots, core_ref[0] == 0, st, gpad, keep_ref, send_ref, W, C)


def inputs_kernel(place_ref, g_ref, x_ref, k_ref, res_ref, *refs):
    pieces, (gpad, acc) = refs[:8], refs[8:]
    Q, W, C = g_ref.shape
    clear_pads(gpad, Q, W, C)
    gpad[:, PAD : PAD + W, :] = g_ref[...]
    signal_grads(0, gpad, k_ref, acc, W, C)

    def pull(q, j):
        inner = (q, pl.ds(PAD + j, ROWS), slice(None))
        outer = (q, pl.ds(j, ROWS), slice(None))
        gpad[inner] = pulled(x_ref[outer], acc[outer], gpad[inner])

    blocks(Q, W, pull)
    for k, piece in enumerate(pieces):
        q = lax.rem(place_ref[0] + k, Q)
        piece[0] = res_ref[q]
        piece[1] = gpad[q, PAD : PAD + W, :]


def spread_kernel(place_ref, g_ref, *pieces):
    Q = len(pieces)
    for k, piece in enumerate(pieces):
        piece[...] = g_ref[lax.rem(place_ref[0] + k, Q)]


def emit_kernel(place_ref, *refs):
    Q = len(refs) - 2
    res_ref, g_ref = refs[Q:]
    for k, piece in enumerate(refs[:Q]):
        q = lax.rem(place_ref[0] + (Q - k), Q)
        res_ref[0, q] = piece[0]
        g_ref[0, q] = piece[1]


def call(kernel, out_shape, n_smem, n_vmem, scratch, gflops, vmem=24):
    return pl.pallas_call(
        kernel,
        out_shape=out_shape,
        in_specs=[SMEM] * n_smem + [VMEM] * n_vmem,
        out_specs=jax.tree.map(lambda _: VMEM, out_shape),
        scratch_shapes=scratch,
        compiler_params=pltpu.CompilerParams(vmem_limit_bytes=vmem << 20),
        cost_estimate=pl.CostEstimate(flops=int(gflops * 1e9), bytes_accessed=4 << 20, transcendentals=0),
    )


def shape(dims, dtype):
    return jax.ShapeDtypeStruct(tuple(dims), dtype)


def sum_kernel(parts_ref, out_ref):
    n = parts_ref.shape[0]
    total = parts_ref[0].astype(F32)
    for i in range(1, n):
        total = total + parts_ref[i].astype(F32)
    total = total.astype(BF16)
    for i in range(n):
        out_ref[i] = total


def summed(parts):
    return call(sum_kernel, shape(parts.shape, BF16), 0, 1, [], 0.01, 8)(parts)


def combine_kernel(keep_a, recv_a, keep_b, recv_b, out_ref):
    split = keep_a.shape[0]
    out_ref[:split] = (keep_a[...] + recv_a[...].astype(F32)).astype(BF16)
    out_ref[split:] = (keep_b[...] + recv_b[...].astype(F32)).astype(BF16)


def tap_slots(W):
    high, low = slots_of((1, 2), W), slots_of((0,), W)
    base = chunk_rows((1, 2), W) // 256
    taps = [(l, a, c) for l in range(3) for a in range(3) for c in range(3)]
    return [high[t] if t in high else base + low[t] if t in low else None for t in taps]


def runs_of(slots):
    runs = []
    for tap, slot in enumerate(slots):
        if slot is None:
            continue
        if runs and runs[-1][0] + runs[-1][2] == tap and runs[-1][1] + runs[-1][2] == slot:
            runs[-1][2] += 1
        else:
            runs.append([tap, slot, 1])
    return runs


def finish_edges_kernel(edges, out_ref, zeros, sem):
    zeros[...] = jnp.zeros_like(zeros)
    copies = [pltpu.make_async_copy(zeros, out_ref.at[t], sem.at[i]) for i, t in enumerate(edges)]
    for copy in copies:
        copy.start()
    for copy in copies:
        copy.wait()


def finish_half_kernel(groups, other, core_ref, rows_ref, grads_ref, out_ref, buf, sem):
    half = 128
    core = core_ref[0]
    place = pl.multiple_of((1 - core if other else core) * half, half)
    copies = []
    for i, (tap, slot, count) in enumerate(groups):
        for s in range(slot, slot + count):
            for lane in range(2):
                rows = rows_ref[s * 256 + lane * half : s * 256 + lane * half + half, :]
                buf[s, :, lane * half : lane * half + half] = rows.astype(F32)
        copy = pltpu.make_async_copy(buf.at[slot : slot + count],
                                     out_ref.at[tap : tap + count, pl.ds(place, half)], sem.at[i])
        copy.start()
        copies.append(copy)
    for copy in copies:
        copy.wait()


def finish_edges(W, C):
    edges = [t for t, slot in enumerate(tap_slots(W)) if slot is None]
    return pl.pallas_call(
        functools.partial(finish_edges_kernel, edges),
        out_shape=shape((27, C, C), F32),
        out_specs=pl.BlockSpec(memory_space=pl.ANY),
        scratch_shapes=[pltpu.VMEM((C, C), F32), pltpu.SemaphoreType.DMA((max(1, len(edges)),))],
        compiler_params=pltpu.CompilerParams(vmem_limit_bytes=4 << 20),
        cost_estimate=pl.CostEstimate(flops=10**6, bytes_accessed=2 << 20, transcendentals=0),
        name="finish_edges",
    )()


def finish_half(core, rows, grads, W, C, other):
    groups = []
    for tap, slot, count in runs_of(tap_slots(W)):
        groups += [(tap + i, slot + i, min(3, count - i)) for i in range(0, count, 3)]
    return pl.pallas_call(
        functools.partial(finish_half_kernel, groups, other),
        out_shape=shape((27, C, C), F32),
        in_specs=[SMEM, VMEM, pl.BlockSpec(memory_space=pl.ANY)],
        out_specs=pl.BlockSpec(memory_space=pl.ANY),
        input_output_aliases={2: 0},
        scratch_shapes=[pltpu.VMEM((rows.shape[0] // 256, 128, C), F32), pltpu.SemaphoreType.DMA((len(groups),))],
        compiler_params=pltpu.CompilerParams(vmem_limit_bytes=12 << 20),
        cost_estimate=pl.CostEstimate(flops=10**6, bytes_accessed=4 << 20, transcendentals=0),
        name="finish_other" if other else "finish_mine",
    )(core, rows, grads)


def run_forward(x, kernels):
    Q, W, C = x.shape
    cells = shape((Q, W, C), BF16)
    return call(forward_kernel, (cells, cells, cells, shape((3, C, Q * W), BF16)), 0, 2,
                [pltpu.VMEM((Q, W + 2 * PAD, C), BF16), pltpu.VMEM((Q, W, C), F32)], 2.0)(x, kernels)


def run_backward(core, place, pieces, x1, x2, st, kernels, factor):
    Q, W, C = x1.shape
    rows = chunk_rows((1, 2), W)
    return call(functools.partial(backward_kernel, factor),
                (shape((Q, W, C), BF16), shape((rows, 128), F32), shape((rows, 128), BF16)), 2, 12,
                [pltpu.VMEM((Q, W + 2 * PAD, C), BF16), pltpu.VMEM((Q, W, C), F32)],
                2.4)(core, place, *pieces, x1, x2, st, kernels)


def run_weights(core, g, st, factor):
    Q, W, C = g.shape
    rows = chunk_rows((0,), W)
    return call(functools.partial(weights_kernel, factor),
                (shape((rows, 128), F32), shape((rows, 128), BF16)), 1, 2,
                [pltpu.VMEM((Q, W + 2 * PAD, C), BF16)], 1.2)(core, g, st)


def run_inputs(place, g, x, kernels, res):
    Q, W, C = g.shape
    return call(inputs_kernel, (shape((2, W, C), BF16),) * Q, 1, 4,
                [pltpu.VMEM((Q, W + 2 * PAD, C), BF16), pltpu.VMEM((Q, W, C), F32)], 1.2)(place, g, x, kernels, res)


def run_spread(place, g):
    Q, W, C = g.shape
    return call(spread_kernel, (shape((W, C), BF16),) * Q, 1, 1, [], 0.01, 4)(place, g)


def run_emit(place, pieces):
    Q, (_, W, C) = len(pieces), pieces[0].shape
    return call(emit_kernel, (shape((1, Q, W, C), BF16),) * 2, 1, Q, [], 0.01, 8)(place, *pieces)


def run_combine(keep_a, recv_a, keep_b, recv_b):
    rows = keep_a.shape[0] + keep_b.shape[0]
    return call(combine_kernel, shape((rows, 128), BF16), 0, 4, [], 0.01, 8)(keep_a, recv_a, keep_b, recv_b)


def all_to_all(value, axes):
    return lax.all_to_all(value, axes, 0, 0, tiled=True)


def swap_cores(value):
    return lax.ppermute(value, "core", [(0, 1), (1, 0)])


def pass_on(pieces):
    Q = len(pieces)
    moved = [lax.ppermute(pieces[k], GROUP, [(i, (i + k) % Q) for i in range(Q)]) for k in range(1, Q)]
    return [pieces[0]] + moved


def local(features, kernels, cotangent):
    _, rows, W, C = features.shape
    core = lax.axis_index("core").reshape(1)
    place = lax.axis_index(GROUP).reshape(1)
    factor = 1.0 / math.sqrt(rows * W * 128)
    x = all_to_all(features[0], GROUP)
    g = run_spread(place, cotangent[0])
    g = pass_on(g)
    res, x1, x2, st = run_forward(x, kernels)
    g1, keep_a, send_a = run_backward(core, place, g, x1, x2, st, kernels, factor)
    recv_a = swap_cores(send_a)
    keep_b, send_b = run_weights(core, g1, st, factor)
    recv_b = swap_cores(send_b)
    parts = run_combine(keep_a, recv_a, keep_b, recv_b).reshape(64, -1, 128)
    parts = all_to_all(parts, CHIPS)
    outs = run_inputs(place, g1, x, kernels, res)
    outs = pass_on(outs)
    parts = summed(parts)
    mine = all_to_all(parts, CHIPS).reshape(-1, 128)
    res, g0 = run_emit(place, outs)
    grads = finish_edges(W, C)
    other = swap_cores(mine)
    grads = finish_half(core, mine, grads, W, C, False)
    grads = finish_half(core, other, grads, W, C, True)
    return res, g0, grads.reshape(3, 3, 3, C, C)


def solution(mesh):
    fine = Mesh(mesh.devices.reshape(2, 4, 4, 2, 2), ("yh", "z", "x", "yl", "core"))
    cells = P(("yl", "core"), ("yh", "z", "x"), None, None)
    return jax.shard_map(
        local,
        mesh=fine,
        in_specs=(cells, P(), cells),
        out_specs=(cells, cells, P()),
        check_vma=False,
    )
```

```python
import functools
import math

import jax
import jax.numpy as jnp
from jax import lax
from jax.experimental import pallas as pl
from jax.experimental.pallas import tpu as pltpu
from jax.sharding import Mesh
from jax.sharding import PartitionSpec as P


GROUP = ("yh", "z")
CHIPS = ("yh", "z", "x", "yl")
BF16 = jnp.bfloat16
F32 = jnp.float32
PAD = 64
ROWS = 128
UNROLL = 8
VMEM = pl.BlockSpec(memory_space=pltpu.VMEM)
SMEM = pl.BlockSpec(memory_space=pltpu.SMEM)


def taps_of(layer, width):
    return [c for c in range(3) if abs(c - 1) * (32 << layer) < width]


def slots_of(layers, width):
    order = [(l, a, c) for l in layers for a in range(3) for c in taps_of(l, width)]
    return {tap: place for place, tap in enumerate(order)}


def chunk_rows(layers, width):
    rows = 256 * len(slots_of(layers, width))
    return -(-rows // 512) * 512


def blocks(Q, W, body):
    per_q = W // ROWS

    def step(i, carry):
        body(i // per_q, pl.multiple_of((i % per_q) * ROWS, ROWS))
        return carry

    lax.fori_loop(0, Q * per_q, step, 0, unroll=UNROLL)


def normed(x):
    x = x.astype(F32)
    r = lax.rsqrt(jnp.mean(x * x, axis=-1, keepdims=True) + 1e-05)
    n = x * r
    return r, n, 0.5 + 0.5 * jnp.tanh(0.5 * n)


def signal_of(x):
    _, n, s = normed(x)
    return (n * s).astype(BF16)


def clear_pads(buf, Q, W, C):
    zeros = jnp.zeros((Q, PAD, C), BF16)
    buf[:, 0:PAD, :] = zeros
    buf[:, PAD + W :, :] = zeros


class Kernels:
    def __init__(self, layers, ref, width):
        self.ref, self.slots = ref, slots_of(layers, width)

    def __getitem__(self, index):
        return self.ref[self.slots[index]]


def copies_of(layers, k_hbm, ref, sem, W):
    return [pltpu.make_async_copy(k_hbm.at[tap], ref.at[slot], sem.at[slot])
            for tap, slot in slots_of(layers, W).items()]


def bring_kernel(W, k_hbm, low_ref, sem):
    copies = copies_of((0,), k_hbm, low_ref, sem, W)
    for copy in copies:
        copy.start()
    for copy in copies:
        copy.wait()


def gather_pieces(place_ref, own, recv, dest, start, W):
    yh, z = lax.shift_right_logical(place_ref[0], 2), lax.bitwise_and(place_ref[0], 3)
    for k in range(4):
        from_z = lax.bitwise_and(z + 4 - k, 3)
        dest[yh * 4 + from_z, start : start + W, :] = own[k]
        dest[(1 - yh) * 4 + from_z, start : start + W, :] = recv[k]


def forward_kernel(place_ref, own, recv, low_ref, k_hbm, res_ref, x_ref, x1, x2, st, high_ref, spad, acc, sem):
    Q, W, C = x_ref.shape
    copies = copies_of((1, 2), k_hbm, high_ref, sem, W)
    for copy in copies:
        copy.start()
    gather_pieces(place_ref, own, recv, x_ref, 0, W)
    low, high = Kernels((0,), low_ref, W), Kernels((1, 2), high_ref, W)
    clear_pads(spad, Q, W, C)
    xs = [x_ref, x1, x2]

    def activate(q, j):
        spad[q, pl.ds(PAD + j, ROWS), :] = signal_of(x_ref[q, pl.ds(j, ROWS), :])

    blocks(Q, W, activate)
    for layer in range(3):
        D = 1 << layer
        k_ref = high if layer else low
        if layer == 1:
            for copy in copies:
                copy.wait()
        for a in (1, 0, 2):
            dq = (a - 1) * D
            q0, nq = max(0, -dq), Q - abs(dq)
            cs = taps_of(layer, W)
            lhs = [spad[q0 + dq : q0 + dq + nq, PAD + (c - 1) * 32 * D : PAD + (c - 1) * 32 * D + W, :].reshape(nq * W, C) for c in cs]
            total = jnp.dot(jnp.concatenate(lhs, axis=1), jnp.concatenate([k_ref[layer, a, c] for c in cs], axis=0),
                            preferred_element_type=F32)
            total = total.reshape(nq, W, C)
            if a == 1:
                acc[...] = total
            else:
                acc[q0 : q0 + nq] += total
        for q in range(Q):
            st[layer, :, q * W : (q + 1) * W] = jnp.transpose(spad[q, PAD : PAD + W, :])

        def update(q, j, layer=layer):
            x = xs[layer][q, pl.ds(j, ROWS), :].astype(F32)
            new = (x + acc[q, pl.ds(j, ROWS), :]).astype(BF16)
            if layer < 2:
                xs[layer + 1][q, pl.ds(j, ROWS), :] = new
                spad[q, pl.ds(PAD + j, ROWS), :] = signal_of(new)
            else:
                res_ref[q, pl.ds(j, ROWS), :] = new

        blocks(Q, W, update)


def shifted_grad(gpad, layer, a, c, W, C):
    Q = gpad.shape[0]
    dq = (a - 1) << layer
    q0, nq = max(0, dq), Q - abs(dq)
    j0 = PAD - (c - 1) * (32 << layer)
    return q0, nq, gpad[q0 - dq : q0 - dq + nq, j0 : j0 + W, :].reshape(nq * W, C)


def weight_grads(factor, layer, slots, first, st, gpad, keep_ref, send_ref, W, C):
    half = C // 2
    for a in range(3):
        for c in taps_of(layer, W):
            q0, nq, shifted = shifted_grad(gpad, layer, a, c, W, C)
            grad = jnp.dot(st[layer, :, q0 * W : (q0 + nq) * W], shifted,
                           preferred_element_type=F32) * factor
            keep = jnp.where(first, grad[:half], grad[half:])
            send = jnp.where(first, grad[half:], grad[:half]).astype(BF16)
            row = slots[layer, a, c] * 256
            keep_ref[row : row + half, :] = keep[:, :128]
            keep_ref[row + half : row + 256, :] = keep[:, 128:]
            send_ref[row : row + half, :] = send[:, :128]
            send_ref[row + half : row + 256, :] = send[:, 128:]


def signal_grads(layer, gpad, k_ref, acc, W, C):
    for a in (1, 0, 2):
        cs = taps_of(layer, W)
        shifted = [shifted_grad(gpad, layer, a, c, W, C) for c in cs]
        q0, nq, _ = shifted[0]
        total = lax.dot_general(jnp.concatenate([s for _, _, s in shifted], axis=1),
                                jnp.concatenate([k_ref[layer, a, c] for c in cs], axis=1),
                                (((1,), (1,)), ((), ())), preferred_element_type=F32)
        total = total.reshape(nq, W, C)
        if a == 1:
            acc[...] = total
        else:
            acc[q0 : q0 + nq] += total


def pulled(x, acc, g):
    r, n, s = normed(x)
    dn = acc * (s * (1.0 + n * (1.0 - s)))
    dx = r * (dn - n * jnp.mean(n * dn, axis=-1, keepdims=True))
    return (g.astype(F32) + dx).astype(BF16)


def clear_tail(slots, keep_ref, send_ref):
    used = 256 * len(slots)
    rest = keep_ref.shape[0] - used
    if rest:
        keep_ref[used:, :] = jnp.zeros((rest, 128), F32)
        send_ref[used:, :] = jnp.zeros((rest, 128), BF16)


def backward_kernel(factor, core_ref, place_ref, *refs):
    own, recv, x1, x2, st, high_ref, next_ref, keep_ref, send_ref, gpad, acc = refs
    Q, W, C = x1.shape
    k_ref = Kernels((1, 2), high_ref, W)
    clear_pads(gpad, Q, W, C)
    gather_pieces(place_ref, own, recv, gpad, PAD, W)
    first = core_ref[0] == 0
    slots = slots_of((1, 2), W)
    clear_tail(slots, keep_ref, send_ref)
    for layer in (2, 1):
        weight_grads(factor, layer, slots, first, st, gpad, keep_ref, send_ref, W, C)
        signal_grads(layer, gpad, k_ref, acc, W, C)
        xl = x2 if layer == 2 else x1

        def pull(q, j, layer=layer, xl=xl):
            inner = (q, pl.ds(PAD + j, ROWS), slice(None))
            outer = (q, pl.ds(j, ROWS), slice(None))
            new = pulled(xl[outer], acc[outer], gpad[inner])
            if layer == 2:
                gpad[inner] = new
            else:
                next_ref[outer] = new

        blocks(Q, W, pull)


def weights_kernel(factor, core_ref, g_ref, st, keep_ref, send_ref, gpad):
    Q, W, C = g_ref.shape
    clear_pads(gpad, Q, W, C)
    gpad[:, PAD : PAD + W, :] = g_ref[...]
    slots = slots_of((0,), W)
    clear_tail(slots, keep_ref, send_ref)
    weight_grads(factor, 0, slots, core_ref[0] == 0, st, gpad, keep_ref, send_ref, W, C)


def inputs_kernel(place_ref, g_ref, x_ref, k_hbm, res_ref, *refs):
    pieces, (gpad, acc, low_ref, sem) = refs[:8], refs[8:]
    Q, W, C = g_ref.shape
    copies = copies_of((0,), k_hbm, low_ref, sem, W)
    for copy in copies:
        copy.start()
    k_ref = Kernels((0,), low_ref, W)
    clear_pads(gpad, Q, W, C)
    gpad[:, PAD : PAD + W, :] = g_ref[...]
    for copy in copies:
        copy.wait()
    signal_grads(0, gpad, k_ref, acc, W, C)

    def pull(q, j):
        inner = (q, pl.ds(PAD + j, ROWS), slice(None))
        outer = (q, pl.ds(j, ROWS), slice(None))
        gpad[inner] = pulled(x_ref[outer], acc[outer], gpad[inner])

    blocks(Q, W, pull)
    for k, piece in enumerate(pieces):
        q = lax.rem(place_ref[0] + k, Q)
        piece[0] = res_ref[q]
        piece[1] = gpad[q, PAD : PAD + W, :]


def spread_kernel(place_ref, x_hbm, *refs):
    pieces, sem = refs[:4], refs[4]
    z = lax.bitwise_and(place_ref[0], 3)
    copies = []
    for k, piece in enumerate(pieces):
        to_z = lax.bitwise_and(z + k, 3)
        for yh in range(2):
            copy = pltpu.make_async_copy(x_hbm.at[yh * 4 + to_z], piece.at[yh], sem.at[2 * k + yh])
            copy.start()
            copies.append(copy)
    for copy in copies:
        copy.wait()


def regroup_kernel(place_ref, *refs):
    own, send = refs[4:]
    yh = lax.shift_right_logical(place_ref[0], 2)
    for k, piece in enumerate(refs[:4]):
        own[k] = piece[yh]
        send[k] = piece[1 - yh]


def emit_kernel(place_ref, *refs):
    Q = len(refs) - 2
    res_ref, g_ref = refs[Q:]
    for k, piece in enumerate(refs[:Q]):
        q = lax.rem(place_ref[0] + (Q - k), Q)
        res_ref[0, q] = piece[0]
        g_ref[0, q] = piece[1]


def call(kernel, out_shape, n_smem, n_vmem, scratch, gflops, vmem=16, hbm=None):
    in_specs = [SMEM] * n_smem + [VMEM] * n_vmem
    if hbm is not None:
        in_specs[hbm] = pl.BlockSpec(memory_space=pltpu.HBM)
    return pl.pallas_call(
        kernel,
        out_shape=out_shape,
        in_specs=in_specs,
        out_specs=jax.tree.map(lambda _: VMEM, out_shape),
        scratch_shapes=scratch,
        compiler_params=pltpu.CompilerParams(vmem_limit_bytes=vmem << 20),
        cost_estimate=pl.CostEstimate(flops=int(gflops * 1e9), bytes_accessed=4 << 20, transcendentals=0),
    )


def shape(dims, dtype):
    return jax.ShapeDtypeStruct(tuple(dims), dtype)


def sum_kernel(parts_ref, out_ref):
    n = parts_ref.shape[0]
    total = parts_ref[0].astype(F32)
    for i in range(1, n):
        total = total + parts_ref[i].astype(F32)
    total = total.astype(BF16)
    for i in range(n):
        out_ref[i] = total


def summed(parts):
    return call(sum_kernel, shape(parts.shape, BF16), 0, 1, [], 0.01, 8)(parts)


def combine_kernel(keep_a, recv_a, keep_b, recv_b, out_ref):
    split = keep_a.shape[0]
    out_ref[:split] = (keep_a[...] + recv_a[...].astype(F32)).astype(BF16)
    out_ref[split:] = (keep_b[...] + recv_b[...].astype(F32)).astype(BF16)


def tap_slots(W):
    high, low = slots_of((1, 2), W), slots_of((0,), W)
    base = chunk_rows((1, 2), W) // 256
    taps = [(l, a, c) for l in range(3) for a in range(3) for c in range(3)]
    return [high[t] if t in high else base + low[t] if t in low else None for t in taps]


def runs_of(slots):
    runs = []
    for tap, slot in enumerate(slots):
        if slot is None:
            continue
        if runs and runs[-1][0] + runs[-1][2] == tap and runs[-1][1] + runs[-1][2] == slot:
            runs[-1][2] += 1
        else:
            runs.append([tap, slot, 1])
    return runs


def finish_edges_kernel(edges, out_ref, zeros, sem):
    zeros[...] = jnp.zeros_like(zeros)
    copies = [pltpu.make_async_copy(zeros, out_ref.at[t], sem.at[i]) for i, t in enumerate(edges)]
    for copy in copies:
        copy.start()
    for copy in copies:
        copy.wait()


def finish_half_kernel(groups, other, core_ref, rows_ref, grads_ref, out_ref, buf, sem):
    half = 128
    core = core_ref[0]
    place = pl.multiple_of((1 - core if other else core) * half, half)
    copies = []
    for i, (tap, slot, count) in enumerate(groups):
        for s in range(slot, slot + count):
            for lane in range(2):
                rows = rows_ref[s * 256 + lane * half : s * 256 + lane * half + half, :]
                buf[s, :, lane * half : lane * half + half] = rows.astype(F32)
        copy = pltpu.make_async_copy(buf.at[slot : slot + count],
                                     out_ref.at[tap : tap + count, pl.ds(place, half)], sem.at[i])
        copy.start()
        copies.append(copy)
    for copy in copies:
        copy.wait()


def finish_edges(W, C):
    edges = [t for t, slot in enumerate(tap_slots(W)) if slot is None]
    return pl.pallas_call(
        functools.partial(finish_edges_kernel, edges),
        out_shape=shape((27, C, C), F32),
        out_specs=pl.BlockSpec(memory_space=pl.ANY),
        scratch_shapes=[pltpu.VMEM((C, C), F32), pltpu.SemaphoreType.DMA((max(1, len(edges)),))],
        compiler_params=pltpu.CompilerParams(vmem_limit_bytes=4 << 20),
        cost_estimate=pl.CostEstimate(flops=10**6, bytes_accessed=2 << 20, transcendentals=0),
        name="finish_edges",
    )()


def finish_half(core, rows, grads, W, C, other):
    groups = []
    for tap, slot, count in runs_of(tap_slots(W)):
        groups += [(tap + i, slot + i, min(3, count - i)) for i in range(0, count, 3)]
    return pl.pallas_call(
        functools.partial(finish_half_kernel, groups, other),
        out_shape=shape((27, C, C), F32),
        in_specs=[SMEM, VMEM, pl.BlockSpec(memory_space=pl.ANY)],
        out_specs=pl.BlockSpec(memory_space=pl.ANY),
        input_output_aliases={2: 0},
        scratch_shapes=[pltpu.VMEM((rows.shape[0] // 256, 128, C), F32), pltpu.SemaphoreType.DMA((len(groups),))],
        compiler_params=pltpu.CompilerParams(vmem_limit_bytes=12 << 20),
        cost_estimate=pl.CostEstimate(flops=10**6, bytes_accessed=4 << 20, transcendentals=0),
        name="finish_other" if other else "finish_mine",
    )(core, rows, grads)


def in_hbm(value):
    return pltpu.with_memory_space_constraint(value, pltpu.HBM)


def run_bring(kernels, W):
    C = kernels.shape[-1]
    low = len(slots_of((0,), W))
    return call(functools.partial(bring_kernel, W), shape((low, C, C), BF16), 0, 1,
                [pltpu.SemaphoreType.DMA((low,))], 0.01, 4, hbm=0)(in_hbm(kernels))


def run_forward(place, own, recv, low, kernels):
    _, W, C = own.shape
    Q = 8
    cells = shape((Q, W, C), BF16)
    high = len(slots_of((1, 2), W))
    outs = (cells, cells, cells, cells, shape((3, C, Q * W), BF16), shape((high, C, C), BF16))
    return call(forward_kernel, outs, 1, 4,
                [pltpu.VMEM((Q, W + 2 * PAD, C), BF16), pltpu.VMEM((Q, W, C), F32),
                 pltpu.SemaphoreType.DMA((high,))], 2.0, hbm=4)(place, own, recv, low, in_hbm(kernels))


def run_backward(core, place, own, recv, x1, x2, st, high, factor):
    Q, W, C = x1.shape
    rows = chunk_rows((1, 2), W)
    return call(functools.partial(backward_kernel, factor),
                (shape((Q, W, C), BF16), shape((rows, 128), F32), shape((rows, 128), BF16)), 2, 6,
                [pltpu.VMEM((Q, W + 2 * PAD, C), BF16), pltpu.VMEM((Q, W, C), F32)],
                2.4)(core, place, own, recv, x1, x2, st, high)


def run_weights(core, g, st, factor):
    Q, W, C = g.shape
    rows = chunk_rows((0,), W)
    return call(functools.partial(weights_kernel, factor),
                (shape((rows, 128), F32), shape((rows, 128), BF16)), 1, 2,
                [pltpu.VMEM((Q, W + 2 * PAD, C), BF16)], 1.2)(core, g, st)


def run_inputs(place, g, x, kernels, res):
    Q, W, C = g.shape
    return call(inputs_kernel, (shape((2, W, C), BF16),) * Q, 1, 4,
                [pltpu.VMEM((Q, W + 2 * PAD, C), BF16), pltpu.VMEM((Q, W, C), F32),
                 pltpu.VMEM((9, C, C), BF16), pltpu.SemaphoreType.DMA((9,))],
                1.2, hbm=3)(place, g, x, in_hbm(kernels), res)


def run_spread(place, x):
    _, W, C = x.shape
    return call(spread_kernel, (shape((2, W, C), BF16),) * 4, 1, 1, [pltpu.SemaphoreType.DMA((8,))],
                0.01, 4, hbm=1)(place, in_hbm(x))


def run_regroup(place, pieces):
    _, W, C = pieces[0].shape
    return call(regroup_kernel, (shape((4, W, C), BF16),) * 2, 1, 4, [], 0.01, 4)(place, *pieces)


def run_emit(place, pieces):
    Q, (_, W, C) = len(pieces), pieces[0].shape
    return call(emit_kernel, (shape((1, Q, W, C), BF16),) * 2, 1, Q, [], 0.01, 8)(place, *pieces)


def run_combine(keep_a, recv_a, keep_b, recv_b):
    rows = keep_a.shape[0] + keep_b.shape[0]
    return call(combine_kernel, shape((rows, 128), BF16), 0, 4, [], 0.01, 8)(keep_a, recv_a, keep_b, recv_b)


def all_to_all(value, axes):
    return lax.all_to_all(value, axes, 0, 0, tiled=True)


def swap_cores(value):
    return lax.ppermute(value, "core", [(0, 1), (1, 0)])


def pass_on(pieces, axes):
    Q = len(pieces)
    moved = [lax.ppermute(pieces[k], axes, [(i, (i + k) % Q) for i in range(Q)]) for k in range(1, Q)]
    return [pieces[0]] + moved


def swap_halves(value):
    return lax.ppermute(value, "yh", [(0, 1), (1, 0)])


def local(features, kernels, cotangent):
    _, rows, W, C = features.shape
    core = lax.axis_index("core").reshape(1)
    place = lax.axis_index(GROUP).reshape(1)
    factor = 1.0 / math.sqrt(rows * W * 128)
    x = run_spread(place, features[0])
    x = pass_on(x, "z")
    g = run_spread(place, cotangent[0])
    g = pass_on(g, "z")
    x_own, x_send = run_regroup(place, x)
    x_recv = swap_halves(x_send)
    low = run_bring(kernels, W)
    g_own, g_send = run_regroup(place, g)
    g_recv = swap_halves(g_send)
    res, x, x1, x2, st, high = run_forward(place, x_own, x_recv, low, kernels)
    g1, keep_a, send_a = run_backward(core, place, g_own, g_recv, x1, x2, st, high, factor)
    recv_a = swap_cores(send_a)
    keep_b, send_b = run_weights(core, g1, st, factor)
    recv_b = swap_cores(send_b)
    parts = run_combine(keep_a, recv_a, keep_b, recv_b).reshape(64, -1, 128)
    parts = all_to_all(parts, CHIPS)
    outs = run_inputs(place, g1, x, kernels, res)
    outs = pass_on(outs, GROUP)
    parts = summed(parts)
    mine = all_to_all(parts, CHIPS).reshape(-1, 128)
    res, g0 = run_emit(place, outs)
    grads = finish_edges(W, C)
    other = swap_cores(mine)
    grads = finish_half(core, mine, grads, W, C, False)
    grads = finish_half(core, other, grads, W, C, True)
    return res, g0, grads.reshape(3, 3, 3, C, C)


def solution(mesh):
    fine = Mesh(mesh.devices.reshape(2, 4, 4, 2, 2), ("yh", "z", "x", "yl", "core"))
    cells = P(("yl", "core"), ("yh", "z", "x"), None, None)
    return jax.shard_map(
        local,
        mesh=fine,
        in_specs=(cells, P(), cells),
        out_specs=(cells, cells, P()),
        check_vma=False,
    )
```

```python
import functools
import math

import jax
import jax.numpy as jnp
from jax import lax
from jax.experimental import pallas as pl
from jax.experimental.pallas import tpu as pltpu
from jax.sharding import Mesh
from jax.sharding import PartitionSpec as P


GROUP = ("yh", "z")
CHIPS = ("yh", "z", "x", "yl")
BF16 = jnp.bfloat16
F32 = jnp.float32
PAD = 64
ROWS = 128
UNROLL = 8
VMEM = pl.BlockSpec(memory_space=pltpu.VMEM)
SMEM = pl.BlockSpec(memory_space=pltpu.SMEM)


def place_of(where_ref):
    return lax.shift_right_logical(where_ref[0], 1)


def core_of(where_ref):
    return lax.bitwise_and(where_ref[0], 1)


def taps_of(layer, width):
    return [c for c in range(3) if abs(c - 1) * (32 << layer) < width]


def slots_of(layers, width):
    order = [(l, a, c) for l in layers for a in range(3) for c in taps_of(l, width)]
    return {tap: place for place, tap in enumerate(order)}


def chunk_rows(layers, width):
    rows = 256 * len(slots_of(layers, width))
    return -(-rows // 512) * 512


def blocks(Q, W, body):
    per_q = W // ROWS

    def step(i, carry):
        body(i // per_q, pl.multiple_of((i % per_q) * ROWS, ROWS))
        return carry

    lax.fori_loop(0, Q * per_q, step, 0, unroll=UNROLL)


def normed(x):
    x = x.astype(F32)
    r = lax.rsqrt(jnp.mean(x * x, axis=-1, keepdims=True) + 1e-05)
    n = x * r
    return r, n, 0.5 + 0.5 * jnp.tanh(0.5 * n)


def signal_of(x):
    _, n, s = normed(x)
    return (n * s).astype(BF16)


def clear_pads(buf, Q, W, C):
    zeros = jnp.zeros((Q, PAD, C), BF16)
    buf[:, 0:PAD, :] = zeros
    buf[:, PAD + W :, :] = zeros


class Kernels:
    def __init__(self, layers, ref, width):
        self.ref, self.slots = ref, slots_of(layers, width)

    def __getitem__(self, index):
        return self.ref[self.slots[index]]


def copies_of(layers, k_hbm, ref, sem, W):
    return [pltpu.make_async_copy(k_hbm.at[tap], ref.at[slot], sem.at[slot])
            for tap, slot in slots_of(layers, W).items()]


def bring_kernel(W, k_hbm, low_ref, high_ref, low_sem, high_sem):
    copies = copies_of((0,), k_hbm, low_ref, low_sem, W) + copies_of((1, 2), k_hbm, high_ref, high_sem, W)
    for copy in copies:
        copy.start()
    for copy in copies:
        copy.wait()


def gather_pieces(place_ref, own, recv, dest, start, W):
    yh, z = lax.shift_right_logical(place_ref[0], 3), lax.bitwise_and(place_of(place_ref), 3)
    for k in range(4):
        from_z = lax.bitwise_and(z + 4 - k, 3)
        dest[yh * 4 + from_z, start : start + W, :] = own[k]
        dest[(1 - yh) * 4 + from_z, start : start + W, :] = recv[k]


def forward_kernel(place_ref, own, recv, low_ref, high_ref, res_ref, x_ref, x1, x2, st, spad, acc):
    Q, W, C = x_ref.shape
    gather_pieces(place_ref, own, recv, x_ref, 0, W)
    low, high = Kernels((0,), low_ref, W), Kernels((1, 2), high_ref, W)
    clear_pads(spad, Q, W, C)
    xs = [x_ref, x1, x2]

    def activate(q, j):
        spad[q, pl.ds(PAD + j, ROWS), :] = signal_of(x_ref[q, pl.ds(j, ROWS), :])

    blocks(Q, W, activate)
    for layer in range(3):
        D = 1 << layer
        k_ref = high if layer else low
        for a in (1, 0, 2):
            dq = (a - 1) * D
            q0, nq = max(0, -dq), Q - abs(dq)
            cs = taps_of(layer, W)
            lhs = [spad[q0 + dq : q0 + dq + nq, PAD + (c - 1) * 32 * D : PAD + (c - 1) * 32 * D + W, :].reshape(nq * W, C) for c in cs]
            total = jnp.dot(jnp.concatenate(lhs, axis=1), jnp.concatenate([k_ref[layer, a, c] for c in cs], axis=0),
                            preferred_element_type=F32)
            total = total.reshape(nq, W, C)
            if a == 1:
                acc[...] = total
            else:
                acc[q0 : q0 + nq] += total
        for q in range(Q):
            st[layer, :, q * W : (q + 1) * W] = jnp.transpose(spad[q, PAD : PAD + W, :])

        def update(q, j, layer=layer):
            x = xs[layer][q, pl.ds(j, ROWS), :].astype(F32)
            new = (x + acc[q, pl.ds(j, ROWS), :]).astype(BF16)
            if layer < 2:
                xs[layer + 1][q, pl.ds(j, ROWS), :] = new
                spad[q, pl.ds(PAD + j, ROWS), :] = signal_of(new)
            else:
                res_ref[q, pl.ds(j, ROWS), :] = new

        blocks(Q, W, update)


def shifted_grad(gpad, layer, a, c, W, C):
    Q = gpad.shape[0]
    dq = (a - 1) << layer
    q0, nq = max(0, dq), Q - abs(dq)
    j0 = PAD - (c - 1) * (32 << layer)
    return q0, nq, gpad[q0 - dq : q0 - dq + nq, j0 : j0 + W, :].reshape(nq * W, C)


def weight_grads(factor, layer, slots, first, st, gpad, keep_ref, send_ref, W, C):
    half = C // 2
    for a in range(3):
        for c in taps_of(layer, W):
            q0, nq, shifted = shifted_grad(gpad, layer, a, c, W, C)
            grad = jnp.dot(st[layer, :, q0 * W : (q0 + nq) * W], shifted,
                           preferred_element_type=F32) * factor
            keep = jnp.where(first, grad[:half], grad[half:])
            send = jnp.where(first, grad[half:], grad[:half]).astype(BF16)
            row = slots[layer, a, c] * 256
            keep_ref[row : row + half, :] = keep[:, :128]
            keep_ref[row + half : row + 256, :] = keep[:, 128:]
            send_ref[row : row + half, :] = send[:, :128]
            send_ref[row + half : row + 256, :] = send[:, 128:]


def signal_grads(layer, gpad, k_ref, acc, W, C):
    for a in (1, 0, 2):
        cs = taps_of(layer, W)
        shifted = [shifted_grad(gpad, layer, a, c, W, C) for c in cs]
        q0, nq, _ = shifted[0]
        total = lax.dot_general(jnp.concatenate([s for _, _, s in shifted], axis=1),
                                jnp.concatenate([k_ref[layer, a, c] for c in cs], axis=1),
                                (((1,), (1,)), ((), ())), preferred_element_type=F32)
        total = total.reshape(nq, W, C)
        if a == 1:
            acc[...] = total
        else:
            acc[q0 : q0 + nq] += total


def pulled(x, acc, g):
    r, n, s = normed(x)
    dn = acc * (s * (1.0 + n * (1.0 - s)))
    dx = r * (dn - n * jnp.mean(n * dn, axis=-1, keepdims=True))
    return (g.astype(F32) + dx).astype(BF16)


def clear_tail(slots, keep_ref, send_ref):
    used = 256 * len(slots)
    rest = keep_ref.shape[0] - used
    if rest:
        keep_ref[used:, :] = jnp.zeros((rest, 128), F32)
        send_ref[used:, :] = jnp.zeros((rest, 128), BF16)


def backward_kernel(factor, core_ref, place_ref, *refs):
    own, recv, x1, x2, st, high_ref, next_ref, keep_ref, send_ref, gpad, acc = refs
    Q, W, C = x1.shape
    k_ref = Kernels((1, 2), high_ref, W)
    clear_pads(gpad, Q, W, C)
    gather_pieces(place_ref, own, recv, gpad, PAD, W)
    first = core_of(core_ref) == 0
    slots = slots_of((1, 2), W)
    clear_tail(slots, keep_ref, send_ref)
    for layer in (2, 1):
        weight_grads(factor, layer, slots, first, st, gpad, keep_ref, send_ref, W, C)
        signal_grads(layer, gpad, k_ref, acc, W, C)
        xl = x2 if layer == 2 else x1

        def pull(q, j, layer=layer, xl=xl):
            inner = (q, pl.ds(PAD + j, ROWS), slice(None))
            outer = (q, pl.ds(j, ROWS), slice(None))
            new = pulled(xl[outer], acc[outer], gpad[inner])
            if layer == 2:
                gpad[inner] = new
            else:
                next_ref[outer] = new

        blocks(Q, W, pull)


def weights_kernel(factor, core_ref, g_ref, st, keep_ref, send_ref, gpad):
    Q, W, C = g_ref.shape
    clear_pads(gpad, Q, W, C)
    gpad[:, PAD : PAD + W, :] = g_ref[...]
    slots = slots_of((0,), W)
    clear_tail(slots, keep_ref, send_ref)
    weight_grads(factor, 0, slots, core_of(core_ref) == 0, st, gpad, keep_ref, send_ref, W, C)


def inputs_kernel(place_ref, g_ref, x_ref, k_hbm, res_ref, *refs):
    pieces, (gpad, acc, low_ref, sem) = refs[:8], refs[8:]
    Q, W, C = g_ref.shape
    copies = copies_of((0,), k_hbm, low_ref, sem, W)
    for copy in copies:
        copy.start()
    k_ref = Kernels((0,), low_ref, W)
    clear_pads(gpad, Q, W, C)
    gpad[:, PAD : PAD + W, :] = g_ref[...]
    for copy in copies:
        copy.wait()
    signal_grads(0, gpad, k_ref, acc, W, C)

    def pull(q, j):
        inner = (q, pl.ds(PAD + j, ROWS), slice(None))
        outer = (q, pl.ds(j, ROWS), slice(None))
        gpad[inner] = pulled(x_ref[outer], acc[outer], gpad[inner])

    blocks(Q, W, pull)
    for k, piece in enumerate(pieces):
        q = lax.rem(place_of(place_ref) + k, Q)
        piece[0] = res_ref[q]
        piece[1] = gpad[q, PAD : PAD + W, :]


def spread_kernel(place_ref, x_hbm, *refs):
    pieces, sem = refs[:4], refs[4]
    z = lax.bitwise_and(place_of(place_ref), 3)
    copies = []
    for k, piece in enumerate(pieces):
        to_z = lax.bitwise_and(z + k, 3)
        for yh in range(2):
            copy = pltpu.make_async_copy(x_hbm.at[yh * 4 + to_z], piece.at[yh], sem.at[2 * k + yh])
            copy.start()
            copies.append(copy)
    for copy in copies:
        copy.wait()


def regroup_kernel(place_ref, *refs):
    own, send = refs[4:]
    yh = lax.shift_right_logical(place_ref[0], 3)
    for k, piece in enumerate(refs[:4]):
        own[k] = piece[yh]
        send[k] = piece[1 - yh]


def emit_kernel(place_ref, *refs):
    Q = len(refs) - 2
    res_ref, g_ref = refs[Q:]
    for k, piece in enumerate(refs[:Q]):
        q = lax.rem(place_of(place_ref) + (Q - k), Q)
        res_ref[0, q] = piece[0]
        g_ref[0, q] = piece[1]


def call(kernel, out_shape, n_smem, n_vmem, scratch, gflops, vmem=16, hbm=None):
    in_specs = [SMEM] * n_smem + [VMEM] * n_vmem
    if hbm is not None:
        in_specs[hbm] = pl.BlockSpec(memory_space=pltpu.HBM)
    return pl.pallas_call(
        kernel,
        out_shape=out_shape,
        in_specs=in_specs,
        out_specs=jax.tree.map(lambda _: VMEM, out_shape),
        scratch_shapes=scratch,
        compiler_params=pltpu.CompilerParams(vmem_limit_bytes=vmem << 20),
        cost_estimate=pl.CostEstimate(flops=int(gflops * 1e9), bytes_accessed=4 << 20, transcendentals=0),
    )


def shape(dims, dtype):
    return jax.ShapeDtypeStruct(tuple(dims), dtype)


def sum_kernel(parts_ref, out_ref):
    n = parts_ref.shape[0]
    total = parts_ref[0].astype(F32)
    for i in range(1, n):
        total = total + parts_ref[i].astype(F32)
    total = total.astype(BF16)
    for i in range(n):
        out_ref[i] = total


def summed(parts):
    return call(sum_kernel, shape(parts.shape, BF16), 0, 1, [], 0.01, 8)(parts)


def combine_kernel(base, keep, recv, *refs):
    out_ref, buf, sem = refs[-3:]
    rows = keep.shape[0] // 4
    copies = []
    for i in range(4):
        part = slice(i * rows, i * rows + rows)
        buf[part] = (keep[part] + recv[part].astype(F32)).astype(BF16)
        copy = pltpu.make_async_copy(buf.at[part], out_ref.at[base + i * rows : base + i * rows + rows], sem.at[i])
        copy.start()
        copies.append(copy)
    for copy in copies:
        copy.wait()


def tap_slots(W):
    high, low = slots_of((1, 2), W), slots_of((0,), W)
    base = chunk_rows((1, 2), W) // 256
    taps = [(l, a, c) for l in range(3) for a in range(3) for c in range(3)]
    return [high[t] if t in high else base + low[t] if t in low else None for t in taps]


def runs_of(slots):
    runs = []
    for tap, slot in enumerate(slots):
        if slot is None:
            continue
        if runs and runs[-1][0] + runs[-1][2] == tap and runs[-1][1] + runs[-1][2] == slot:
            runs[-1][2] += 1
        else:
            runs.append([tap, slot, 1])
    return runs


def finish_edges_kernel(edges, out_ref, zeros, sem):
    zeros[...] = jnp.zeros_like(zeros)
    copies = [pltpu.make_async_copy(zeros, out_ref.at[t], sem.at[i]) for i, t in enumerate(edges)]
    for copy in copies:
        copy.start()
    for copy in copies:
        copy.wait()


def finish_half_kernel(groups, other, core_ref, rows_ref, grads_ref, out_ref, buf, sem):
    half = 128
    core = core_of(core_ref)
    place = pl.multiple_of((1 - core if other else core) * half, half)
    copies = []
    for i, (tap, slot, count) in enumerate(groups):
        for s in range(slot, slot + count):
            for lane in range(2):
                rows = rows_ref[s * 256 + lane * half : s * 256 + lane * half + half, :]
                buf[s, :, lane * half : lane * half + half] = rows.astype(F32)
        copy = pltpu.make_async_copy(buf.at[slot : slot + count],
                                     out_ref.at[tap : tap + count, pl.ds(place, half)], sem.at[i])
        copy.start()
        copies.append(copy)
    for copy in copies:
        copy.wait()


def finish_edges(W, C):
    edges = [t for t, slot in enumerate(tap_slots(W)) if slot is None]
    return pl.pallas_call(
        functools.partial(finish_edges_kernel, edges),
        out_shape=shape((27, C, C), F32),
        out_specs=pl.BlockSpec(memory_space=pl.ANY),
        scratch_shapes=[pltpu.VMEM((C, C), F32), pltpu.SemaphoreType.DMA((max(1, len(edges)),))],
        compiler_params=pltpu.CompilerParams(vmem_limit_bytes=4 << 20),
        cost_estimate=pl.CostEstimate(flops=10**6, bytes_accessed=2 << 20, transcendentals=0),
        name="finish_edges",
    )()


def finish_half(core, rows, grads, W, C, other):
    groups = []
    for tap, slot, count in runs_of(tap_slots(W)):
        groups += [(tap + i, slot + i, min(3, count - i)) for i in range(0, count, 3)]
    return pl.pallas_call(
        functools.partial(finish_half_kernel, groups, other),
        out_shape=shape((27, C, C), F32),
        in_specs=[SMEM, VMEM, pl.BlockSpec(memory_space=pl.ANY)],
        out_specs=pl.BlockSpec(memory_space=pl.ANY),
        input_output_aliases={2: 0},
        scratch_shapes=[pltpu.VMEM((rows.shape[0] // 256, 128, C), F32), pltpu.SemaphoreType.DMA((len(groups),))],
        compiler_params=pltpu.CompilerParams(vmem_limit_bytes=12 << 20),
        cost_estimate=pl.CostEstimate(flops=10**6, bytes_accessed=4 << 20, transcendentals=0),
        name="finish_other" if other else "finish_mine",
    )(core, rows, grads)


def in_hbm(value):
    return pltpu.with_memory_space_constraint(value, pltpu.HBM)


def run_bring(kernels, W):
    C = kernels.shape[-1]
    low, high = len(slots_of((0,), W)), len(slots_of((1, 2), W))
    return call(functools.partial(bring_kernel, W),
                (shape((low, C, C), BF16), shape((high, C, C), BF16)), 0, 1,
                [pltpu.SemaphoreType.DMA((low,)), pltpu.SemaphoreType.DMA((high,))], 0.01, 4, hbm=0)(in_hbm(kernels))


def run_forward(place, own, recv, low, high):
    _, W, C = own.shape
    Q = 8
    cells = shape((Q, W, C), BF16)
    return call(forward_kernel, (cells, cells, cells, cells, shape((3, C, Q * W), BF16)), 1, 4,
                [pltpu.VMEM((Q, W + 2 * PAD, C), BF16), pltpu.VMEM((Q, W, C), F32)], 2.0)(place, own, recv, low, high)


def run_backward(core, place, own, recv, x1, x2, st, high, factor):
    Q, W, C = x1.shape
    rows = chunk_rows((1, 2), W)
    return call(functools.partial(backward_kernel, factor),
                (shape((Q, W, C), BF16), shape((rows, 128), F32), shape((rows, 128), BF16)), 2, 6,
                [pltpu.VMEM((Q, W + 2 * PAD, C), BF16), pltpu.VMEM((Q, W, C), F32)],
                2.4)(core, place, own, recv, x1, x2, st, high)


def run_weights(core, g, st, factor):
    Q, W, C = g.shape
    rows = chunk_rows((0,), W)
    return call(functools.partial(weights_kernel, factor),
                (shape((rows, 128), F32), shape((rows, 128), BF16)), 1, 2,
                [pltpu.VMEM((Q, W + 2 * PAD, C), BF16)], 1.2)(core, g, st)


def run_inputs(place, g, x, kernels, res):
    Q, W, C = g.shape
    return call(inputs_kernel, (shape((2, W, C), BF16),) * Q, 1, 4,
                [pltpu.VMEM((Q, W + 2 * PAD, C), BF16), pltpu.VMEM((Q, W, C), F32),
                 pltpu.VMEM((9, C, C), BF16), pltpu.SemaphoreType.DMA((9,))],
                1.2, hbm=3)(place, g, x, in_hbm(kernels), res)


def run_spread(place, x):
    _, W, C = x.shape
    return call(spread_kernel, (shape((2, W, C), BF16),) * 4, 1, 1, [pltpu.SemaphoreType.DMA((8,))],
                0.01, 4, hbm=1)(place, in_hbm(x))


def run_regroup(place, pieces):
    _, W, C = pieces[0].shape
    return call(regroup_kernel, (shape((4, W, C), BF16),) * 2, 1, 4, [], 0.01, 4)(place, *pieces)


def run_emit(place, pieces):
    Q, (_, W, C) = len(pieces), pieces[0].shape
    return call(emit_kernel, (shape((1, Q, W, C), BF16),) * 2, 1, Q, [], 0.01, 8)(place, *pieces)


def run_combine(keep, recv, base, total, earlier=None):
    any_space = pl.BlockSpec(memory_space=pl.ANY)
    more = [] if earlier is None else [earlier]
    return pl.pallas_call(
        functools.partial(combine_kernel, base),
        out_shape=shape((total, 128), BF16),
        in_specs=[VMEM, VMEM] + [any_space] * len(more),
        out_specs=any_space,
        input_output_aliases={2: 0} if more else {},
        scratch_shapes=[pltpu.VMEM(keep.shape, BF16), pltpu.SemaphoreType.DMA((4,))],
        compiler_params=pltpu.CompilerParams(vmem_limit_bytes=8 << 20),
        cost_estimate=pl.CostEstimate(flops=10**6, bytes_accessed=2 << 20, transcendentals=0),
        name="combine_b" if more else "combine_a",
    )(keep, recv, *more)


def all_to_all(value, axes):
    return lax.all_to_all(value, axes, 0, 0, tiled=True)


def swap_cores(value):
    return lax.ppermute(value, "core", [(0, 1), (1, 0)])


def pass_on(pieces, axes):
    Q = len(pieces)
    moved = [lax.ppermute(pieces[k], axes, [(i, (i + k) % Q) for i in range(Q)]) for k in range(1, Q)]
    return [pieces[0]] + moved


def swap_halves(value):
    return lax.ppermute(value, "yh", [(0, 1), (1, 0)])


def local(features, kernels, cotangent):
    _, rows, W, C = features.shape
    core = place = lax.axis_index(GROUP + ("core",)).reshape(1)
    factor = 1.0 / math.sqrt(rows * W * 128)
    x = run_spread(place, features[0])
    x = pass_on(x, "z")
    g = run_spread(place, cotangent[0])
    g = pass_on(g, "z")
    x_own, x_send = run_regroup(place, x)
    x_recv = swap_halves(x_send)
    low, high = run_bring(kernels, W)
    g_own, g_send = run_regroup(place, g)
    g_recv = swap_halves(g_send)
    res, x, x1, x2, st = run_forward(place, x_own, x_recv, low, high)
    g1, keep_a, send_a = run_backward(core, place, g_own, g_recv, x1, x2, st, high, factor)
    recv_a = swap_cores(send_a)
    keep_b, send_b = run_weights(core, g1, st, factor)
    recv_b = swap_cores(send_b)
    total = keep_a.shape[0] + keep_b.shape[0]
    parts = run_combine(keep_a, recv_a, 0, total)
    parts = run_combine(keep_b, recv_b, keep_a.shape[0], total, parts).reshape(64, -1, 128)
    parts = all_to_all(parts, CHIPS)
    outs = run_inputs(place, g1, x, kernels, res)
    outs = pass_on(outs, GROUP)
    parts = summed(parts)
    mine = all_to_all(parts, CHIPS).reshape(-1, 128)
    res, g0 = run_emit(place, outs)
    grads = finish_edges(W, C)
    other = swap_cores(mine)
    grads = finish_half(core, mine, grads, W, C, False)
    grads = finish_half(core, other, grads, W, C, True)
    return res, g0, grads.reshape(3, 3, 3, C, C)


def solution(mesh):
    fine = Mesh(mesh.devices.reshape(2, 4, 4, 2, 2), ("yh", "z", "x", "yl", "core"))
    cells = P(("yl", "core"), ("yh", "z", "x"), None, None)
    return jax.shard_map(
        local,
        mesh=fine,
        in_specs=(cells, P(), cells),
        out_specs=(cells, cells, P()),
        check_vma=False,
    )
```

```python
import functools
import math

import jax
import jax.numpy as jnp
from jax import lax
from jax.experimental import pallas as pl
from jax.experimental.pallas import tpu as pltpu
from jax.sharding import Mesh
from jax.sharding import PartitionSpec as P


GROUP = ("yh", "z")
CHIPS = ("yh", "z", "x", "yl")
BF16 = jnp.bfloat16
F32 = jnp.float32
PAD = 64
ROWS = 128
UNROLL = 8
VMEM = pl.BlockSpec(memory_space=pltpu.VMEM)
SMEM = pl.BlockSpec(memory_space=pltpu.SMEM)


def place_of(where_ref):
    return lax.shift_right_logical(where_ref[0], 1)


def core_of(where_ref):
    return lax.bitwise_and(where_ref[0], 1)


def taps_of(layer, width):
    return [c for c in range(3) if abs(c - 1) * (32 << layer) < width]


def slots_of(layers, width):
    order = [(l, a, c) for l in layers for a in range(3) for c in taps_of(l, width)]
    return {tap: place for place, tap in enumerate(order)}


def chunk_rows(layers, width):
    rows = 256 * len(slots_of(layers, width))
    return -(-rows // 512) * 512


def blocks(Q, W, body):
    per_q = W // ROWS

    def step(i, carry):
        body(i // per_q, pl.multiple_of((i % per_q) * ROWS, ROWS))
        return carry

    lax.fori_loop(0, Q * per_q, step, 0, unroll=UNROLL)


def normed(x):
    x = x.astype(F32)
    r = lax.rsqrt(jnp.mean(x * x, axis=-1, keepdims=True) + 1e-05)
    n = x * r
    return r, n, 0.5 + 0.5 * jnp.tanh(0.5 * n)


def signal_of(x):
    _, n, s = normed(x)
    return (n * s).astype(BF16)


def clear_pads(buf, Q, W, C):
    zeros = jnp.zeros((Q, PAD, C), BF16)
    buf[:, 0:PAD, :] = zeros
    buf[:, PAD + W :, :] = zeros


class Kernels:
    def __init__(self, layers, ref, width):
        self.ref, self.slots = ref, slots_of(layers, width)

    def __getitem__(self, index):
        return self.ref[self.slots[index]]


def copies_of(layers, k_hbm, ref, sem, W):
    return [pltpu.make_async_copy(k_hbm.at[tap], ref.at[slot], sem.at[slot])
            for tap, slot in slots_of(layers, W).items()]


def bring_kernel(W, k_hbm, low_ref, high_ref, low_sem, high_sem):
    copies = copies_of((0,), k_hbm, low_ref, low_sem, W) + copies_of((1, 2), k_hbm, high_ref, high_sem, W)
    for copy in copies:
        copy.start()
    for copy in copies:
        copy.wait()


def gather_pieces(place_ref, own, recv, dest, start, W):
    yh, z = lax.shift_right_logical(place_ref[0], 3), lax.bitwise_and(place_of(place_ref), 3)
    for k in range(4):
        from_z = lax.bitwise_and(z + 4 - k, 3)
        dest[yh * 4 + from_z, start : start + W, :] = own[k]
        dest[(1 - yh) * 4 + from_z, start : start + W, :] = recv[k]


def forward_kernel(place_ref, own, recv, low_ref, high_ref, res_ref, x_ref, x1, x2, st, spad, acc):
    Q, W, C = x_ref.shape
    gather_pieces(place_ref, own, recv, x_ref, 0, W)
    low, high = Kernels((0,), low_ref, W), Kernels((1, 2), high_ref, W)
    clear_pads(spad, Q, W, C)
    xs = [x_ref, x1, x2]

    def activate(q, j):
        spad[q, pl.ds(PAD + j, ROWS), :] = signal_of(x_ref[q, pl.ds(j, ROWS), :])

    blocks(Q, W, activate)
    for layer in range(3):
        D = 1 << layer
        k_ref = high if layer else low
        for a in (1, 0, 2):
            dq = (a - 1) * D
            q0, nq = max(0, -dq), Q - abs(dq)
            cs = taps_of(layer, W)
            lhs = [spad[q0 + dq : q0 + dq + nq, PAD + (c - 1) * 32 * D : PAD + (c - 1) * 32 * D + W, :].reshape(nq * W, C) for c in cs]
            total = jnp.dot(jnp.concatenate(lhs, axis=1), jnp.concatenate([k_ref[layer, a, c] for c in cs], axis=0),
                            preferred_element_type=F32)
            total = total.reshape(nq, W, C)
            if a == 1:
                acc[...] = total
            else:
                acc[q0 : q0 + nq] += total
        for q in range(Q):
            st[layer, :, q * W : (q + 1) * W] = jnp.transpose(spad[q, PAD : PAD + W, :])

        def update(q, j, layer=layer):
            x = xs[layer][q, pl.ds(j, ROWS), :].astype(F32)
            new = (x + acc[q, pl.ds(j, ROWS), :]).astype(BF16)
            if layer < 2:
                xs[layer + 1][q, pl.ds(j, ROWS), :] = new
                spad[q, pl.ds(PAD + j, ROWS), :] = signal_of(new)
            else:
                res_ref[q, pl.ds(j, ROWS), :] = new

        blocks(Q, W, update)


def shifted_grad(gpad, layer, a, c, W, C):
    Q = gpad.shape[0]
    dq = (a - 1) << layer
    q0, nq = max(0, dq), Q - abs(dq)
    j0 = PAD - (c - 1) * (32 << layer)
    return q0, nq, gpad[q0 - dq : q0 - dq + nq, j0 : j0 + W, :].reshape(nq * W, C)


def weight_grads(factor, layer, slots, first, st, gpad, keep_ref, send_ref, W, C):
    half = C // 2
    for a in range(3):
        for c in taps_of(layer, W):
            q0, nq, shifted = shifted_grad(gpad, layer, a, c, W, C)
            grad = jnp.dot(st[layer, :, q0 * W : (q0 + nq) * W], shifted,
                           preferred_element_type=F32) * factor
            keep = jnp.where(first, grad[:half], grad[half:])
            send = jnp.where(first, grad[half:], grad[:half]).astype(BF16)
            row = slots[layer, a, c] * 256
            keep_ref[row : row + half, :] = keep[:, :128]
            keep_ref[row + half : row + 256, :] = keep[:, 128:]
            send_ref[row : row + half, :] = send[:, :128]
            send_ref[row + half : row + 256, :] = send[:, 128:]


def signal_grads(layer, gpad, k_ref, acc, W, C):
    for a in (1, 0, 2):
        cs = taps_of(layer, W)
        shifted = [shifted_grad(gpad, layer, a, c, W, C) for c in cs]
        q0, nq, _ = shifted[0]
        total = lax.dot_general(jnp.concatenate([s for _, _, s in shifted], axis=1),
                                jnp.concatenate([k_ref[layer, a, c] for c in cs], axis=1),
                                (((1,), (1,)), ((), ())), preferred_element_type=F32)
        total = total.reshape(nq, W, C)
        if a == 1:
            acc[...] = total
        else:
            acc[q0 : q0 + nq] += total


def pulled(x, acc, g):
    r, n, s = normed(x)
    dn = acc * (s * (1.0 + n * (1.0 - s)))
    dx = r * (dn - n * jnp.mean(n * dn, axis=-1, keepdims=True))
    return (g.astype(F32) + dx).astype(BF16)


def clear_tail(slots, keep_ref, send_ref):
    used = 256 * len(slots)
    rest = keep_ref.shape[0] - used
    if rest:
        keep_ref[used:, :] = jnp.zeros((rest, 128), F32)
        send_ref[used:, :] = jnp.zeros((rest, 128), BF16)


def backward_kernel(factor, core_ref, place_ref, *refs):
    own, recv, x1, x2, st, high_ref, next_ref, keep_ref, send_ref, gpad, acc = refs
    Q, W, C = x1.shape
    k_ref = Kernels((1, 2), high_ref, W)
    clear_pads(gpad, Q, W, C)
    gather_pieces(place_ref, own, recv, gpad, PAD, W)
    first = core_of(core_ref) == 0
    slots = slots_of((1, 2), W)
    clear_tail(slots, keep_ref, send_ref)
    for layer in (2, 1):
        weight_grads(factor, layer, slots, first, st, gpad, keep_ref, send_ref, W, C)
        signal_grads(layer, gpad, k_ref, acc, W, C)
        xl = x2 if layer == 2 else x1

        def pull(q, j, layer=layer, xl=xl):
            inner = (q, pl.ds(PAD + j, ROWS), slice(None))
            outer = (q, pl.ds(j, ROWS), slice(None))
            new = pulled(xl[outer], acc[outer], gpad[inner])
            if layer == 2:
                gpad[inner] = new
            else:
                next_ref[outer] = new

        blocks(Q, W, pull)


def weights_kernel(factor, core_ref, g_ref, st, keep_ref, send_ref, gpad):
    Q, W, C = g_ref.shape
    clear_pads(gpad, Q, W, C)
    gpad[:, PAD : PAD + W, :] = g_ref[...]
    slots = slots_of((0,), W)
    clear_tail(slots, keep_ref, send_ref)
    weight_grads(factor, 0, slots, core_of(core_ref) == 0, st, gpad, keep_ref, send_ref, W, C)


def inputs_kernel(place_ref, g_ref, x_ref, k_hbm, res_ref, *refs):
    pieces, (gpad, acc, low_ref, sem) = refs[:8], refs[8:]
    Q, W, C = g_ref.shape
    copies = copies_of((0,), k_hbm, low_ref, sem, W)
    for copy in copies:
        copy.start()
    k_ref = Kernels((0,), low_ref, W)
    clear_pads(gpad, Q, W, C)
    gpad[:, PAD : PAD + W, :] = g_ref[...]
    for copy in copies:
        copy.wait()
    signal_grads(0, gpad, k_ref, acc, W, C)

    def pull(q, j):
        inner = (q, pl.ds(PAD + j, ROWS), slice(None))
        outer = (q, pl.ds(j, ROWS), slice(None))
        gpad[inner] = pulled(x_ref[outer], acc[outer], gpad[inner])

    blocks(Q, W, pull)
    for k, piece in enumerate(pieces):
        q = lax.rem(place_of(place_ref) + k, Q)
        piece[0] = res_ref[q]
        piece[1] = gpad[q, PAD : PAD + W, :]


def spread_kernel(place_ref, x_hbm, *refs):
    pieces, sem = refs[:4], refs[4]
    z = lax.bitwise_and(place_of(place_ref), 3)
    copies = []
    for k, piece in enumerate(pieces):
        to_z = lax.bitwise_and(z + k, 3)
        for yh in range(2):
            copy = pltpu.make_async_copy(x_hbm.at[yh * 4 + to_z], piece.at[yh], sem.at[2 * k + yh])
            copy.start()
            copies.append(copy)
    for copy in copies:
        copy.wait()


def regroup_kernel(place_ref, *refs):
    own, send = refs[4:]
    yh = lax.shift_right_logical(place_ref[0], 3)
    for k, piece in enumerate(refs[:4]):
        own[k] = piece[yh]
        send[k] = piece[1 - yh]


def emit_kernel(place_ref, *refs):
    Q = len(refs) - 2
    res_ref, g_ref = refs[Q:]
    for k, piece in enumerate(refs[:Q]):
        q = lax.rem(place_of(place_ref) + (Q - k), Q)
        res_ref[0, q] = piece[0]
        g_ref[0, q] = piece[1]


def call(kernel, out_shape, n_smem, n_vmem, scratch, gflops, vmem=16, hbm=None):
    in_specs = [SMEM] * n_smem + [VMEM] * n_vmem
    if hbm is not None:
        in_specs[hbm] = pl.BlockSpec(memory_space=pltpu.HBM)
    return pl.pallas_call(
        kernel,
        out_shape=out_shape,
        in_specs=in_specs,
        out_specs=jax.tree.map(lambda _: VMEM, out_shape),
        scratch_shapes=scratch,
        compiler_params=pltpu.CompilerParams(vmem_limit_bytes=vmem << 20),
        cost_estimate=pl.CostEstimate(flops=int(gflops * 1e9), bytes_accessed=4 << 20, transcendentals=0),
    )


def shape(dims, dtype):
    return jax.ShapeDtypeStruct(tuple(dims), dtype)


def sum_kernel(parts_ref, out_ref, buf, sem):
    n = parts_ref.shape[0]
    total = parts_ref[0].astype(F32)
    for i in range(1, n):
        total = total + parts_ref[i].astype(F32)
    total = total.astype(BF16)
    group = buf.shape[0]
    for i in range(group):
        buf[i] = total
    copies = [pltpu.make_async_copy(buf, out_ref.at[i * group : i * group + group], sem.at[i])
              for i in range(n // group)]
    for copy in copies:
        copy.start()
    for copy in copies:
        copy.wait()


def summed(parts):
    return pl.pallas_call(
        sum_kernel,
        out_shape=shape(parts.shape, BF16),
        in_specs=[VMEM],
        out_specs=pl.BlockSpec(memory_space=pl.ANY),
        scratch_shapes=[pltpu.VMEM((8,) + parts.shape[1:], BF16), pltpu.SemaphoreType.DMA((8,))],
        compiler_params=pltpu.CompilerParams(vmem_limit_bytes=8 << 20),
        cost_estimate=pl.CostEstimate(flops=10**7, bytes_accessed=3 << 20, transcendentals=0),
        name="sum_parts",
    )(parts)


def combine_kernel(base, keep, recv, *refs):
    out_ref, buf, sem = refs[-3:]
    rows = keep.shape[0] // 4
    copies = []
    for i in range(4):
        part = slice(i * rows, i * rows + rows)
        buf[part] = (keep[part] + recv[part].astype(F32)).astype(BF16)
        copy = pltpu.make_async_copy(buf.at[part], out_ref.at[base + i * rows : base + i * rows + rows], sem.at[i])
        copy.start()
        copies.append(copy)
    for copy in copies:
        copy.wait()


def tap_slots(W):
    high, low = slots_of((1, 2), W), slots_of((0,), W)
    base = chunk_rows((1, 2), W) // 256
    taps = [(l, a, c) for l in range(3) for a in range(3) for c in range(3)]
    return [high[t] if t in high else base + low[t] if t in low else None for t in taps]


def runs_of(slots):
    runs = []
    for tap, slot in enumerate(slots):
        if slot is None:
            continue
        if runs and runs[-1][0] + runs[-1][2] == tap and runs[-1][1] + runs[-1][2] == slot:
            runs[-1][2] += 1
        else:
            runs.append([tap, slot, 1])
    return runs


def finish_edges_kernel(edges, out_ref, zeros, sem):
    zeros[...] = jnp.zeros_like(zeros)
    copies = [pltpu.make_async_copy(zeros, out_ref.at[t], sem.at[i]) for i, t in enumerate(edges)]
    for copy in copies:
        copy.start()
    for copy in copies:
        copy.wait()


def finish_half_kernel(groups, other, core_ref, rows_ref, grads_ref, out_ref, buf, sem):
    half = 128
    core = core_of(core_ref)
    place = pl.multiple_of((1 - core if other else core) * half, half)
    copies = []
    for i, (tap, slot, count) in enumerate(groups):
        for s in range(slot, slot + count):
            for lane in range(2):
                rows = rows_ref[s * 256 + lane * half : s * 256 + lane * half + half, :]
                buf[s, :, lane * half : lane * half + half] = rows.astype(F32)
        copy = pltpu.make_async_copy(buf.at[slot : slot + count],
                                     out_ref.at[tap : tap + count, pl.ds(place, half)], sem.at[i])
        copy.start()
        copies.append(copy)
    for copy in copies:
        copy.wait()


def finish_edges(W, C):
    edges = [t for t, slot in enumerate(tap_slots(W)) if slot is None]
    return pl.pallas_call(
        functools.partial(finish_edges_kernel, edges),
        out_shape=shape((27, C, C), F32),
        out_specs=pl.BlockSpec(memory_space=pl.ANY),
        scratch_shapes=[pltpu.VMEM((C, C), F32), pltpu.SemaphoreType.DMA((max(1, len(edges)),))],
        compiler_params=pltpu.CompilerParams(vmem_limit_bytes=4 << 20),
        cost_estimate=pl.CostEstimate(flops=10**6, bytes_accessed=2 << 20, transcendentals=0),
        name="finish_edges",
    )()


def finish_half(core, rows, grads, W, C, other):
    groups = []
    for tap, slot, count in runs_of(tap_slots(W)):
        groups += [(tap + i, slot + i, 1) for i in range(count)]
    return pl.pallas_call(
        functools.partial(finish_half_kernel, groups, other),
        out_shape=shape((27, C, C), F32),
        in_specs=[SMEM, VMEM, pl.BlockSpec(memory_space=pl.ANY)],
        out_specs=pl.BlockSpec(memory_space=pl.ANY),
        input_output_aliases={2: 0},
        scratch_shapes=[pltpu.VMEM((rows.shape[0] // 256, 128, C), F32), pltpu.SemaphoreType.DMA((len(groups),))],
        compiler_params=pltpu.CompilerParams(vmem_limit_bytes=12 << 20),
        cost_estimate=pl.CostEstimate(flops=10**6, bytes_accessed=4 << 20, transcendentals=0),
        name="finish_other" if other else "finish_mine",
    )(core, rows, grads)


def in_hbm(value):
    return pltpu.with_memory_space_constraint(value, pltpu.HBM)


def run_bring(kernels, W):
    C = kernels.shape[-1]
    low, high = len(slots_of((0,), W)), len(slots_of((1, 2), W))
    return call(functools.partial(bring_kernel, W),
                (shape((low, C, C), BF16), shape((high, C, C), BF16)), 0, 1,
                [pltpu.SemaphoreType.DMA((low,)), pltpu.SemaphoreType.DMA((high,))], 0.01, 4, hbm=0)(in_hbm(kernels))


def run_forward(place, own, recv, low, high):
    _, W, C = own.shape
    Q = 8
    cells = shape((Q, W, C), BF16)
    return call(forward_kernel, (cells, cells, cells, cells, shape((3, C, Q * W), BF16)), 1, 4,
                [pltpu.VMEM((Q, W + 2 * PAD, C), BF16), pltpu.VMEM((Q, W, C), F32)], 2.0)(place, own, recv, low, high)


def run_backward(core, place, own, recv, x1, x2, st, high, factor):
    Q, W, C = x1.shape
    rows = chunk_rows((1, 2), W)
    return call(functools.partial(backward_kernel, factor),
                (shape((Q, W, C), BF16), shape((rows, 128), F32), shape((rows, 128), BF16)), 2, 6,
                [pltpu.VMEM((Q, W + 2 * PAD, C), BF16), pltpu.VMEM((Q, W, C), F32)],
                2.4)(core, place, own, recv, x1, x2, st, high)


def run_weights(core, g, st, factor):
    Q, W, C = g.shape
    rows = chunk_rows((0,), W)
    return call(functools.partial(weights_kernel, factor),
                (shape((rows, 128), F32), shape((rows, 128), BF16)), 1, 2,
                [pltpu.VMEM((Q, W + 2 * PAD, C), BF16)], 1.2)(core, g, st)


def run_inputs(place, g, x, kernels, res):
    Q, W, C = g.shape
    return call(inputs_kernel, (shape((2, W, C), BF16),) * Q, 1, 4,
                [pltpu.VMEM((Q, W + 2 * PAD, C), BF16), pltpu.VMEM((Q, W, C), F32),
                 pltpu.VMEM((9, C, C), BF16), pltpu.SemaphoreType.DMA((9,))],
                1.2, hbm=3)(place, g, x, in_hbm(kernels), res)


def run_spread(place, x):
    _, W, C = x.shape
    return call(spread_kernel, (shape((2, W, C), BF16),) * 4, 1, 1, [pltpu.SemaphoreType.DMA((8,))],
                0.01, 4, hbm=1)(place, in_hbm(x))


def run_regroup(place, pieces):
    _, W, C = pieces[0].shape
    return call(regroup_kernel, (shape((4, W, C), BF16),) * 2, 1, 4, [], 0.01, 4)(place, *pieces)


def run_emit(place, pieces):
    Q, (_, W, C) = len(pieces), pieces[0].shape
    return call(emit_kernel, (shape((1, Q, W, C), BF16),) * 2, 1, Q, [], 0.01, 8)(place, *pieces)


def run_combine(keep, recv, base, total, earlier=None):
    any_space = pl.BlockSpec(memory_space=pl.ANY)
    more = [] if earlier is None else [earlier]
    return pl.pallas_call(
        functools.partial(combine_kernel, base),
        out_shape=shape((total, 128), BF16),
        in_specs=[VMEM, VMEM] + [any_space] * len(more),
        out_specs=any_space,
        input_output_aliases={2: 0} if more else {},
        scratch_shapes=[pltpu.VMEM(keep.shape, BF16), pltpu.SemaphoreType.DMA((4,))],
        compiler_params=pltpu.CompilerParams(vmem_limit_bytes=8 << 20),
        cost_estimate=pl.CostEstimate(flops=10**6, bytes_accessed=2 << 20, transcendentals=0),
        name="combine_b" if more else "combine_a",
    )(keep, recv, *more)


def all_to_all(value, axes):
    return lax.all_to_all(value, axes, 0, 0, tiled=True)


def swap_cores(value):
    return lax.ppermute(value, "core", [(0, 1), (1, 0)])


def pass_on(pieces, axes):
    Q = len(pieces)
    moved = [lax.ppermute(pieces[k], axes, [(i, (i + k) % Q) for i in range(Q)]) for k in range(1, Q)]
    return [pieces[0]] + moved


def swap_halves(value):
    return lax.ppermute(value, "yh", [(0, 1), (1, 0)])


def local(features, kernels, cotangent):
    _, rows, W, C = features.shape
    core = place = lax.axis_index(GROUP + ("core",)).reshape(1)
    factor = 1.0 / math.sqrt(rows * W * 128)
    x = run_spread(place, features[0])
    x = pass_on(x, "z")
    g = run_spread(place, cotangent[0])
    g = pass_on(g, "z")
    x_own, x_send = run_regroup(place, x)
    x_recv = swap_halves(x_send)
    low, high = run_bring(kernels, W)
    g_own, g_send = run_regroup(place, g)
    g_recv = swap_halves(g_send)
    res, x, x1, x2, st = run_forward(place, x_own, x_recv, low, high)
    g1, keep_a, send_a = run_backward(core, place, g_own, g_recv, x1, x2, st, high, factor)
    recv_a = swap_cores(send_a)
    keep_b, send_b = run_weights(core, g1, st, factor)
    recv_b = swap_cores(send_b)
    total = keep_a.shape[0] + keep_b.shape[0]
    parts = run_combine(keep_a, recv_a, 0, total)
    parts = run_combine(keep_b, recv_b, keep_a.shape[0], total, parts).reshape(64, -1, 128)
    parts = all_to_all(parts, CHIPS)
    outs = run_inputs(place, g1, x, kernels, res)
    outs = pass_on(outs, GROUP)
    parts = summed(parts)
    mine = all_to_all(parts, CHIPS).reshape(-1, 128)
    res, g0 = run_emit(place, outs)
    grads = finish_edges(W, C)
    other = swap_cores(mine)
    grads = finish_half(core, mine, grads, W, C, False)
    grads = finish_half(core, other, grads, W, C, True)
    return res, g0, grads.reshape(3, 3, 3, C, C)


def solution(mesh):
    fine = Mesh(mesh.devices.reshape(2, 4, 4, 2, 2), ("yh", "z", "x", "yl", "core"))
    cells = P(("yl", "core"), ("yh", "z", "x"), None, None)
    return jax.shard_map(
        local,
        mesh=fine,
        in_specs=(cells, P(), cells),
        out_specs=(cells, cells, P()),
        check_vma=False,
    )
```
